256 devices in a mesh: batch: 128 (over y, z, x), tile: 2 (over core).
Axes of the slice: x: 4, y: 4, z: 8, core: 2. Of those that a mesh axis runs over, the one named last changes fastest.
Arguments:
- first_view: bfloat16 [256, 8192], P('batch'), may hold values from -1500 to 1500
- second_view: bfloat16 [256, 8192], P('batch'), may hold values from -1500 to 1500
Outputs:
- grad_first: bfloat16 [256, 8192], P('batch', 'tile')
- grad_second: bfloat16 [256, 8192], P('batch', 'tile')
The draws below stay inside these ranges and needn't reach their ends.
All inputs are finite; a program needn't handle non-finite values.
Results may differ from the reference program's by a relative error of at most 0.0043.
Values may be sent and summed in bfloat16 or wider, within the bound.
A program may use at most 64 MiB of HBM per device.

```python
import math
import jax
import jax.numpy as jnp
from jax import lax

D = 8192
BATCH = 256


def view_pair(key):
    keys = jax.random.split(jax.random.fold_in(key, 11), 10)
    shared = jax.random.truncated_normal(keys[0], -4.0, 4.0, (BATCH, 1), jnp.float32)
    noise_one = jax.random.truncated_normal(keys[1], -4.0, 4.0, (BATCH, D), jnp.float32)
    noise_two = jax.random.truncated_normal(keys[2], -4.0, 4.0, (BATCH, D), jnp.float32)
    rise = math.log(10.0)
    place = jnp.arange(BATCH, dtype=jnp.float32) / BATCH
    row_scale = jnp.exp(rise * place[:, None] + jax.random.uniform(keys[3], (BATCH, 1), jnp.float32, -0.35, 0.35))
    load_one = jax.random.uniform(keys[4], (1, D), jnp.float32, 0.15, 0.45)
    load_two = jax.random.uniform(keys[5], (1, D), jnp.float32, 0.15, 0.45)
    scale_one = jnp.exp(jax.random.uniform(keys[6], (1, D), jnp.float32, 0.0, math.log(10.0)))
    scale_two = jnp.exp(jax.random.uniform(keys[7], (1, D), jnp.float32, 0.0, math.log(10.0)))
    offset_one = jax.random.uniform(keys[8], (1, D), jnp.float32, -2.0, 2.0)
    offset_two = jax.random.uniform(keys[9], (1, D), jnp.float32, -2.0, 2.0)
    first = scale_one * (offset_one + row_scale * (load_one * shared + noise_one))
    second = scale_two * (offset_two + row_scale * (load_two * shared + 0.6 * noise_one + 0.8 * noise_two))
    return (first, second)


def draw_first_view(key, part):
    first, second = view_pair(key)
    return first.astype(jnp.bfloat16)


def draw_second_view(key, part):
    first, second = view_pair(key)
    return second.astype(jnp.bfloat16)


def setup_inputs(seed: int = 0) -> dict:
    seeds = jax.random.split(jax.random.key(seed), 3)
    return {
        "first_view": draw_first_view(jax.random.fold_in(seeds[2], 71), 0),
        "second_view": draw_second_view(jax.random.fold_in(seeds[2], 71), 0),
    }


epsilon = 1e-05
decorrelation = 0.0051

def normalized(view, total_rows):
    values = view.astype(jnp.float32)
    mean_value = lax.optimization_barrier(jnp.sum(values, 0)) / total_rows
    variance = lax.optimization_barrier(jnp.sum(values * values, 0)) / total_rows - mean_value * mean_value
    inverse = lax.rsqrt(variance + epsilon)
    return (((values - mean_value) * inverse).astype(jnp.bfloat16), inverse)

def reference(first_view, second_view):
    total_rows, feature_width = first_view.shape
    norm_first, inverse_first = normalized(first_view, total_rows)
    norm_second, inverse_second = normalized(second_view, total_rows)
    block_width = math.gcd(feature_width, 512)
    block_count = feature_width // block_width
    first_blocks = norm_first.reshape(total_rows, block_count, block_width).transpose(1, 0, 2)

    def step_block(carry, inputs):
        pull_second, stat_second = carry
        first_block, block_index = inputs
        correlation = lax.dot_general(first_block, norm_second, (((0,), (0,)), ((), ())), preferred_element_type=jnp.float32) / total_rows
        row_ids = block_index * block_width + lax.iota(jnp.int32, block_width)
        col_ids = lax.iota(jnp.int32, feature_width)
        diagonal = row_ids[:, None] == col_ids[None, :]
        slope_tile = jnp.where(diagonal, correlation - 1.0, decorrelation * correlation).astype(jnp.bfloat16)
        weighted = slope_tile.astype(jnp.float32) * correlation
        pull_block = lax.dot_general(norm_second, slope_tile, (((1,), (1,)), ((), ())), preferred_element_type=jnp.float32)
        pull_second = pull_second + jnp.dot(first_block, slope_tile, preferred_element_type=jnp.float32)
        stat_second = stat_second + lax.optimization_barrier(jnp.sum(weighted, 0))
        return ((pull_second, stat_second), (pull_block, lax.optimization_barrier(jnp.sum(weighted, 1))))
    start_carry = (jnp.zeros((total_rows, feature_width), jnp.float32), jnp.zeros((feature_width,), jnp.float32))
    indices = jnp.arange(block_count, dtype=jnp.int32)
    (pull_second, stat_second), (pull_blocks, stat_blocks) = lax.scan(step_block, start_carry, (first_blocks, indices))
    pull_first = pull_blocks.transpose(1, 0, 2).reshape(total_rows, feature_width)
    stat_first = stat_blocks.reshape(feature_width)
    grad_first = (inverse_first * (pull_first - norm_first.astype(jnp.float32) * stat_first)).astype(jnp.bfloat16)
    grad_second = (inverse_second * (pull_second - norm_second.astype(jnp.float32) * stat_second)).astype(jnp.bfloat16)
    return (grad_first, grad_second)
```

```python
import jax
import jax.numpy as jnp
from jax import lax
from jax.sharding import PartitionSpec as P

BAND = 16


epsilon = 1e-05
decorrelation = 0.0051


def fold_rows(received, row_count, row_groups, group_size, block_width):
    return (
        received.reshape(row_count, row_groups, group_size, block_width)
        .sum(2)
        .reshape(row_count, row_groups * block_width)
    )


def fold_cols(received, row_count, row_groups, group_size, block_width):
    return (
        received.reshape(row_count, row_groups, group_size, block_width)
        .sum(1)
        .reshape(row_count, group_size * block_width)
    )


def normalized(whole, total_rows):
    values = whole.astype(jnp.float32)
    mean_value = jnp.sum(values, 0) / total_rows
    variance = jnp.sum(values * values, 0) / total_rows - mean_value * mean_value
    inverse = lax.rsqrt(variance + epsilon)
    return ((values - mean_value) * inverse).astype(jnp.bfloat16), inverse


def per_device(first_view, second_view):
    row_count, feature_width = first_view.shape
    device_count = lax.axis_size("batch")
    band_index = lax.axis_index("batch")
    tile_index = lax.axis_index("tile")
    total_rows = row_count * device_count
    group_size = BAND
    row_groups = device_count // group_size
    block_rows = feature_width * group_size // device_count
    block_cols = feature_width // (2 * group_size)
    row_band = band_index // group_size
    column_block = band_index % group_size + group_size * tile_index
    send_first = jnp.broadcast_to(
        first_view.reshape(row_count, row_groups, 1, block_rows),
        (row_count, row_groups, group_size, block_rows),
    ).reshape(row_count, device_count * block_rows)
    picked = lax.dynamic_slice_in_dim(
        second_view.reshape(row_count, 2, group_size, block_cols), tile_index, 1, 1
    )
    send_second = jnp.broadcast_to(picked, (row_count, row_groups, group_size, block_cols)).reshape(
        row_count, device_count * block_cols
    )
    whole_first, whole_second = (
        lax.all_to_all(send_first, "batch", split_axis=1, concat_axis=0, tiled=True),
        lax.all_to_all(send_second, "batch", split_axis=1, concat_axis=0, tiled=True),
    )
    norm_first, inverse_first = normalized(whole_first, total_rows)
    norm_second, inverse_second = normalized(whole_second, total_rows)
    correlation = (
        lax.dot_general(
            norm_first, norm_second, (((0,), (0,)), ((), ())), preferred_element_type=jnp.float32
        )
        / total_rows
    )
    row_ids = row_band * block_rows + lax.iota(jnp.int32, block_rows)
    col_ids = column_block * block_cols + lax.iota(jnp.int32, block_cols)
    on_diagonal = row_ids[:, None] == col_ids[None, :]
    slope_tile = jnp.where(on_diagonal, correlation - 1.0, decorrelation * correlation).astype(
        jnp.bfloat16
    )
    weighted = slope_tile.astype(jnp.float32) * correlation
    stat_first = jnp.sum(weighted, 1)
    stat_second = jnp.sum(weighted, 0)
    pull_first = lax.dot_general(
        norm_second, slope_tile, (((1,), (1,)), ((), ())), preferred_element_type=jnp.float32
    )
    pull_second = jnp.dot(norm_first, slope_tile, preferred_element_type=jnp.float32)
    part_first = inverse_first * (pull_first - norm_first.astype(jnp.float32) * stat_first)
    part_second = inverse_second * (pull_second - norm_second.astype(jnp.float32) * stat_second)
    back_first, back_second = (
        lax.all_to_all(part_first, "batch", split_axis=0, concat_axis=1, tiled=True),
        lax.all_to_all(part_second, "batch", split_axis=0, concat_axis=1, tiled=True),
    )
    full_first = fold_rows(back_first, row_count, row_groups, group_size, block_rows)
    grad_second = fold_cols(back_second, row_count, row_groups, group_size, block_cols)
    grad_first = lax.psum_scatter(full_first, "tile", scatter_dimension=1, tiled=True)
    return (grad_first.astype(jnp.bfloat16), grad_second.astype(jnp.bfloat16))


def solution(mesh):
    return jax.shard_map(
        per_device,
        mesh=mesh,
        in_specs=(P("batch", None), P("batch", None)),
        out_specs=(P("batch", "tile"), P("batch", "tile")),
        check_vma=False,
    )
```
